128 devices in a mesh: view: 16 (over y, z), depth: 8 (over x, core).
Axes of the slice: x: 4, y: 4, z: 4, core: 2. Of those that a mesh axis runs over, the one named last changes fastest.
Arguments:
- features: bfloat16 [48, 1024, 32], P('view'), may hold values from -6 to 6
- view_lists: int32 [48, 10], P('view'), may hold values from 0 to 31
- requests: int32 [16, 16, 2], replicated, may hold values from 0 to 2
- warp_idx: int32 [48, 10, 64, 8, 128], P('view', None, None, 'depth'), may hold values from -682 to 1023
- conv_weight: bfloat16 [27, 8, 8], replicated, may hold values from -0.4375 to 0.4375
Outputs:
- regularized: bfloat16 [48, 8, 64, 8, 128], P('view', None, 'depth')
The draws below stay inside these ranges and needn't reach their ends.
Inputs may be any that keep to these rules, and one draw needn't show every extreme that they name: `warp_idx`: A negative entry marks a sample that falls outside the source tile and is left out of the sum and the count.
All inputs are finite; a program needn't handle non-finite values.
Results may differ from the reference program's by a relative error of at most 0.0049.
Values may be sent and summed in bfloat16 or wider, within the bound.
No kernel may reach another device: no remote copies, remote signals or barrier semaphores. Data moves between devices by JAX's collectives and lax.ppermute only.
A program may use at most 128 MiB of HBM per device.

```python
import jax
import jax.numpy as jnp
from jax import lax

CHANNELS = 32
GROUPS = 8
DEPTH = 64
SOURCES = 10
CAP = 2
TILE_H = 8
TILE_W = 128
VIEW_DEV = 3
VIEWS = 48
PIX = 1024
N_VIEW = 16


def with_ends(values, key, smallest, top_value):
    spot = [jax.random.randint(jax.random.fold_in(key, axis), (), 0, length) for axis, length in enumerate(values.shape)]
    widest = values.shape.index(max(values.shape))
    beside = spot[:widest] + [(spot[widest] + 1) % values.shape[widest]] + spot[widest + 1:]
    return values.at[tuple(spot)].set(smallest).at[tuple(beside)].set(top_value)


def levels(stream_key, dims, shards, smallest, high):
    level = 1.0
    for position, shards_of in shards:
        draws = jax.random.uniform(jax.random.fold_in(jax.random.fold_in(stream_key, 6), position), (shards_of,), jnp.float32, smallest / len(shards), high / len(shards))
        level = level * jnp.repeat(jnp.exp(draws), dims[position] // shards_of).reshape((-1,) + (1,) * (len(dims) - 1 - position))
    return level


def noise(rng, dims, width, bound, pieces=(), held_as=jnp.bfloat16):
    array = jax.random.normal(rng, dims, jnp.float32) * width
    if len(pieces) > 0:
        array = levels(rng, dims, pieces, -0.22, 0.18) * array
    return jnp.clip(array, min=-bound, max=bound).astype(held_as)


def setup_inputs(seed: int = 0) -> dict:
    key_of = jax.random.split(jax.random.key(seed), 6)
    features = noise(key_of[0], (VIEWS, PIX, CHANNELS), 1.0, 6.0, ((0, 16),))
    view_lists = with_ends(jax.random.randint(key_of[1], (VIEWS, SOURCES), 0, N_VIEW * CAP), jax.random.fold_in(key_of[1], 1), 0, (N_VIEW * CAP) - 1).astype(jnp.int32)
    requests = with_ends(jax.random.randint(key_of[2], (N_VIEW, N_VIEW, CAP), 0, VIEW_DEV), jax.random.fold_in(key_of[2], 1), 0, VIEW_DEV - 1).astype(jnp.int32)
    warp_idx = with_ends(jax.random.randint(key_of[3], (VIEWS, SOURCES, DEPTH, TILE_H, TILE_W), 0 - (2 * PIX) // 3, PIX), jax.random.fold_in(key_of[3], 1), 0 - (2 * PIX) // 3, PIX - 1).astype(jnp.int32)
    conv_weight = noise(key_of[4], (27, GROUPS, GROUPS), (27 * GROUPS) ** -0.5, 0.4375)
    return dict(features=features, view_lists=view_lists, requests=requests, warp_idx=warp_idx, conv_weight=conv_weight)


def reference(features, view_lists, requests, warp_idx, conv_weight):
    views = features.shape[0]
    owner_dev = view_lists // CAP
    slot_index = view_lists % CAP
    asker = (jnp.arange(views, dtype=jnp.int32) // VIEW_DEV).astype(jnp.int32)[:, None]
    source = (owner_dev * VIEW_DEV + requests[asker, owner_dev, slot_index]).astype(jnp.int32)
    flat_pool = features.reshape(views * PIX, CHANNELS)

    def one_view(item):
        own_tile, warp_rows, source_ids = item
        usable = warp_rows >= 0
        picks = (source_ids[:, None, None, None] * PIX + jnp.maximum(warp_rows, 0)).astype(jnp.int32)
        warped = jnp.take(flat_pool, picks.reshape(-1), axis=0)
        warped = warped.reshape(SOURCES, DEPTH, PIX, GROUPS, CHANNELS // GROUPS).astype(jnp.float32)
        own_groups = own_tile.reshape(PIX, GROUPS, CHANNELS // GROUPS).astype(jnp.float32)
        products = jnp.einsum('sdpgk,pgk->sdpg', warped, own_groups)
        usable_flat = usable.reshape(SOURCES, DEPTH, PIX)
        masked = jnp.where(usable_flat[..., None], products, jnp.float32(0.0))
        live_count = jnp.sum(usable_flat.astype(jnp.float32), axis=0)
        corr = 0.5 * jnp.sum(masked, axis=0) / jnp.maximum(live_count, jnp.float32(1.0))[..., None]
        corr = jnp.transpose(corr, (2, 0, 1)).reshape(GROUPS, DEPTH, TILE_H, TILE_W)
        return corr.astype(jnp.bfloat16)

    cost = lax.map(one_view, (features, warp_idx, source))
    padded = jnp.pad(cost, ((0, 0), (0, 0), (1, 1), (1, 1), (1, 1)))
    summed = jnp.zeros((views, GROUPS, DEPTH, TILE_H, TILE_W), jnp.float32)
    for depth_tap in range(3):
        for row_tap in range(3):
            for col_tap in range(3):
                shifted = padded[:, :, depth_tap:depth_tap + DEPTH, row_tap:row_tap + TILE_H, col_tap:col_tap + TILE_W]
                kernel = conv_weight[9 * depth_tap + 3 * row_tap + col_tap].astype(jnp.float32)
                summed = summed + jnp.einsum('vgdhw,gk->vkdhw', shifted.astype(jnp.float32), kernel)
    return summed.astype(jnp.bfloat16)
```

```python
import functools

import jax
import jax.numpy as jnp
from jax import lax
from jax.experimental import pallas as pl
from jax.experimental.pallas import tpu as pltpu
from jax.sharding import PartitionSpec as P

LOW = 256


def cost_kernel(source_ref, here_ref, warp_ref, own_ref, pool_ref, out_ref, low_ref, high_ref, scale_ref, sums_ref):
    view = pl.program_id(0)
    sources, planes, columns = warp_ref.shape[1:]
    channels = own_ref.shape[1]
    slabs = out_ref.shape[0]
    groups = out_ref.shape[3]
    slab = planes // slabs
    block = 4
    warp = warp_ref[0]
    outside = warp < 0
    low_ref[...] = jnp.where(outside, -1, warp & (LOW - 1)).astype(jnp.float32)
    high_ref[...] = warp >> 8
    live = jnp.sum(jnp.where(outside, 0.0, 1.0), axis=0)
    scale_ref[...] = 0.5 / jnp.maximum(live, 1.0)
    tiles = LOW // 16
    pixel = lax.broadcasted_iota(jnp.int32, (tiles, 16, columns), 0) * 16 + lax.broadcasted_iota(
        jnp.int32, (tiles, 16, columns), 1
    )
    pixel = pixel.astype(jnp.float32).astype(jnp.bfloat16)
    one = jnp.ones((), jnp.bfloat16)
    zero = jnp.zeros((), jnp.bfloat16)
    own = own_ref[0].astype(jnp.float32)

    def planes_of(start):
        totals = [jnp.zeros((channels, columns), jnp.float32) for _ in range(block)]
        for s in range(sources):
            tile = pool_ref[source_ref[view, s]]
            lhs = jnp.concatenate([tile[:, h * LOW : (h + 1) * LOW] for h in range(4)], axis=0)
            hots = []
            for j in range(block):
                row = jnp.broadcast_to(low_ref[s, pl.ds(start + j, 1), :], (16, columns)).astype(jnp.bfloat16)
                hots.append(jnp.where(pixel == row[None], one, zero).reshape(LOW, columns))
            picked = jnp.dot(lhs, jnp.concatenate(hots, axis=1), preferred_element_type=jnp.float32)
            for j in range(block):
                high = jnp.broadcast_to(high_ref[s, pl.ds(start + j, 1), :], (channels, columns))
                odd = (high & 1) == 1
                upper = (high & 2) == 2
                part = picked[:, j * columns : (j + 1) * columns]
                q = [part[h * channels : (h + 1) * channels] for h in range(4)]
                totals[j] = totals[j] + jnp.where(upper, jnp.where(odd, q[3], q[2]), jnp.where(odd, q[1], q[0]))
        costs = []
        for j in range(block):
            sums_ref[j] = totals[j] * own
            size = channels // groups
            corr = sums_ref[j, pl.ds(0, groups, stride=size), :]
            for n in range(1, size):
                corr = corr + sums_ref[j, pl.ds(n, groups, stride=size), :]
            corr = corr * jnp.broadcast_to(scale_ref[pl.ds(start + j, 1), :], (groups, columns))
            costs.append(corr.astype(jnp.bfloat16))
        return costs

    out_ref[0, 0, 0] = jnp.zeros((groups, columns), jnp.bfloat16)
    out_ref[slabs - 1, 0, slab + 1] = jnp.zeros((groups, columns), jnp.bfloat16)

    def step(half, carry):
        t = half // 2
        inner = (half % 2) * block
        costs = planes_of(half * block)
        for j in range(block):
            out_ref[t, 0, 1 + inner + j] = costs[j]

        @pl.when((inner == 0) & (t > 0))
        def _():
            out_ref[t - 1, 0, slab + 1] = costs[0]

        @pl.when((inner > 0) & (t < slabs - 1))
        def _():
            out_ref[t + 1, 0, 0] = costs[block - 1]

        return carry

    lax.fori_loop(0, planes // block, step, 0)


def cost_slabs(source_ids, here, warp, tiles, pool, slabs, groups):
    views, sources, planes, columns = warp.shape
    channels = tiles.shape[1]
    slab = planes // slabs
    return pl.pallas_call(
        cost_kernel,
        grid_spec=pltpu.PrefetchScalarGridSpec(
            num_scalar_prefetch=2,
            grid=(views,),
            in_specs=[
                pl.BlockSpec((1, sources, planes, columns), lambda v, s, h: (v, 0, 0, 0)),
                pl.BlockSpec((1, channels, columns), lambda v, s, h: (v, 0, h[0])),
                pl.BlockSpec(pool.shape, lambda v, s, h: (0, 0, 0), pipeline_mode=pl.Buffered(1)),
            ],
            out_specs=pl.BlockSpec((slabs, 1, slab + 2, groups, columns), lambda v, s, h: (0, v, 0, 0, 0)),
            scratch_shapes=[
                pltpu.VMEM((sources, planes, columns), jnp.float32),
                pltpu.VMEM((sources, planes, columns), jnp.int32),
                pltpu.VMEM((planes, columns), jnp.float32),
                pltpu.VMEM((4, channels, columns), jnp.float32),
            ],
        ),
        out_shape=jax.ShapeDtypeStruct((slabs, views, slab + 2, groups, columns), jnp.bfloat16),
        name="cost",
    )(source_ids, here, warp, tiles, pool)


def mix_kernel(weight_ref, slab_ref, out_ref, rows_ref):
    rows, _, padded, groups, columns = slab_ref.shape
    planes = padded - 2
    lane = lax.broadcasted_iota(jnp.int32, (groups, columns), 1)
    blank = jnp.zeros((groups, columns), jnp.float32)
    empty = jnp.zeros((4 * groups, columns), jnp.bfloat16)
    weight = weight_ref[...]
    terms = []
    for d in range(padded):
        taps = []
        for i in range(rows):
            cell = slab_ref[i, 0, d].astype(jnp.float32)
            left = jnp.where(lane == 0, 0.0, pltpu.roll(cell, 1, 1))
            right = jnp.where(lane == columns - 1, 0.0, pltpu.roll(cell, columns - 1, 1))
            taps.append(jnp.concatenate([left, cell, right, blank], axis=0).astype(jnp.bfloat16))
        above = jnp.concatenate([empty] + taps[:-1], axis=1)
        below = jnp.concatenate(taps[1:] + [empty], axis=1)
        matrix = jnp.concatenate([above, jnp.concatenate(taps, axis=1), below], axis=0)
        terms.append(jnp.dot(weight, matrix, preferred_element_type=jnp.float32))
        if d >= 2:
            mixed = terms[d - 2][0:groups] + terms[d - 1][groups : 2 * groups] + terms[d][2 * groups : 3 * groups]
            for i in range(rows):
                rows_ref[pl.ds(i, groups, stride=rows), :] = mixed[:, i * columns : (i + 1) * columns]
            for h in range(groups):
                out_ref[0, h, d - 2] = rows_ref[h * rows : (h + 1) * rows, :].astype(jnp.bfloat16)


def mix_slabs(weight, slabs):
    rows, views, padded, groups, columns = slabs.shape
    return pl.pallas_call(
        mix_kernel,
        grid=(views,),
        in_specs=[
            pl.BlockSpec(weight.shape, lambda v: (0, 0)),
            pl.BlockSpec((rows, 1, padded, groups, columns), lambda v: (0, v, 0, 0, 0)),
        ],
        out_specs=pl.BlockSpec((1, groups, padded - 2, rows, columns), lambda v: (v, 0, 0, 0, 0)),
        out_shape=jax.ShapeDtypeStruct((views, groups, padded - 2, rows, columns), jnp.bfloat16),
        scratch_shapes=[pltpu.VMEM((groups * rows, columns), jnp.float32)],
        name="mix",
    )(weight, slabs)


def on_device(features, view_lists, requests, warp_idx, conv_weight):
    view_here = lax.axis_index("view")
    depth_here = lax.axis_index("depth")
    depth_count = lax.axis_size("depth")
    local_views = features.shape[0]
    groups = conv_weight.shape[1]
    asked = requests.shape[2]
    tiles = jnp.transpose(features, (0, 2, 1))
    pool = lax.all_gather(tiles, "view", axis=0, tiled=True)
    owner_dev = view_lists // asked
    slot_index = view_lists % asked
    source_ids = owner_dev * local_views + requests[view_here, owner_dev, slot_index]
    warp = warp_idx.reshape(warp_idx.shape[:3] + warp_idx.shape[4:])
    slabs = cost_slabs(source_ids, depth_here.reshape(1), warp, tiles, pool, depth_count, groups)
    slabs = lax.all_to_all(slabs, "depth", split_axis=0, concat_axis=0, tiled=True)
    taps = conv_weight.reshape(3, 3, 3 * groups, groups)
    taps = jnp.pad(taps, ((0, 0), (0, 0), (0, groups), (0, 0)))
    weight = jnp.transpose(taps, (0, 3, 1, 2)).reshape(3 * groups, 12 * groups)
    return mix_slabs(weight, slabs)


def solution(mesh):
    return jax.shard_map(
        on_device,
        mesh=mesh,
        in_specs=(
            P("view", None, None),
            P("view", None),
            P(),
            P("view", None, None, "depth", None),
            P(),
        ),
        out_specs=P("view", None, "depth", None, None),
        check_vma=False,
    )
```

```python
import functools

import jax
import jax.numpy as jnp
from jax import lax
from jax.experimental import pallas as pl
from jax.experimental.pallas import tpu as pltpu
from jax.sharding import PartitionSpec as P

LOW = 256
BLOCK = 4


def ask_kernel(requests_ref, tiles_ref, out_ref):
    here = lax.axis_index("view")
    half = out_ref.shape[3]
    start = pl.multiple_of((lax.axis_index("depth") % 2) * half, half)
    for u in range(out_ref.shape[0]):
        for c in range(out_ref.shape[1]):
            out_ref[u, c] = tiles_ref[requests_ref[u, c, here], :, pl.ds(start, half)]


def asked_tiles(requests, tiles):
    askers, slots, _ = requests.shape
    _, channels, pixels = tiles.shape
    return pl.pallas_call(
        ask_kernel,
        in_specs=[pl.BlockSpec(memory_space=pltpu.SMEM), pl.BlockSpec(memory_space=pltpu.VMEM)],
        out_specs=pl.BlockSpec(memory_space=pltpu.VMEM),
        out_shape=jax.ShapeDtypeStruct((askers, slots, channels, pixels // 2), jnp.bfloat16),
        name="ask",
    )(requests, tiles)


def pack_kernel(warp_ref, out_ref):
    slabs, views, sources, slab, _ = out_ref.shape
    for v in range(views):
        for s in range(sources):
            for t in range(slabs):
                out_ref[t, v, s] = warp_ref[v, s, t * slab : (t + 1) * slab].astype(jnp.int16)


def packed_warp(warp, slabs):
    views, sources, planes, columns = warp.shape
    return pl.pallas_call(
        pack_kernel,
        in_specs=[pl.BlockSpec(memory_space=pltpu.VMEM)],
        out_specs=pl.BlockSpec(memory_space=pltpu.VMEM),
        out_shape=jax.ShapeDtypeStruct((slabs, views, sources, planes // slabs, columns), jnp.int16),
        cost_estimate=pl.CostEstimate(flops=warp.size, bytes_accessed=warp.size * 6, transcendentals=0),
        name="pack",
    )(warp)


def cost_kernel(slot_ref, warp_ref, own_ref, near_ref, far_ref, out_ref, low_ref, high_ref, scale_ref, sums_ref, *, chosen):
    view = pl.program_id(0)
    rows, _, sources, _, columns = warp_ref.shape
    channels = own_ref.shape[1]
    groups = out_ref.shape[3]
    size = channels // groups
    count = len(chosen)
    flip = (lax.axis_index("depth") % 2) * 2
    for i in range(rows):
        live = jnp.zeros((warp_ref.shape[3], columns), jnp.float32)
        for s in range(sources):
            warp = warp_ref[i, 0, s].astype(jnp.int32)
            outside = warp < 0
            low_ref[s, i] = jnp.where(outside, -1, warp & (LOW - 1)).astype(jnp.float32)
            high_ref[s, i] = (warp >> 8) ^ flip
            live = live + jnp.where(outside, 0.0, 1.0)
        scale_ref[i] = 0.5 / jnp.maximum(live, 1.0)
    tiles = LOW // 16
    pixel = lax.broadcasted_iota(jnp.int32, (tiles, 16, columns), 0) * 16 + lax.broadcasted_iota(
        jnp.int32, (tiles, 16, columns), 1
    )
    pixel = pixel.astype(jnp.float32).astype(jnp.bfloat16)
    one = jnp.ones((), jnp.bfloat16)
    zero = jnp.zeros((), jnp.bfloat16)

    def cells_of(cells):
        totals = [jnp.zeros((channels, columns), jnp.float32) for _ in cells]
        for s in range(sources):
            slot = slot_ref[view, s]
            near = near_ref[slot]
            far = far_ref[slot]
            lhs = jnp.concatenate([near[:, :LOW], near[:, LOW:], far[:, :LOW], far[:, LOW:]], axis=0)
            hots = []
            for i, d in cells:
                row = jnp.broadcast_to(low_ref[s, i, pl.ds(d, 1), :], (16, columns)).astype(jnp.bfloat16)
                hots.append(jnp.where(pixel == row[None], one, zero).reshape(LOW, columns))
            picked = jnp.dot(lhs, jnp.concatenate(hots, axis=1), preferred_element_type=jnp.float32)
            for j, (i, d) in enumerate(cells):
                high = jnp.broadcast_to(high_ref[s, i, pl.ds(d, 1), :], (channels, columns))
                odd = (high & 1) == 1
                upper = (high & 2) == 2
                part = picked[:, j * columns : (j + 1) * columns]
                q = [part[h * channels : (h + 1) * channels] for h in range(4)]
                totals[j] = totals[j] + jnp.where(upper, jnp.where(odd, q[3], q[2]), jnp.where(odd, q[1], q[0]))
        for j, (i, d) in enumerate(cells):
            own = own_ref[0, :, pl.ds(pl.multiple_of(i * columns, columns), columns)].astype(jnp.float32)
            sums_ref[j] = totals[j] * own
            corr = sums_ref[j, pl.ds(0, groups, stride=size), :]
            for n in range(1, size):
                corr = corr + sums_ref[j, pl.ds(n, groups, stride=size), :]
            corr = corr * jnp.broadcast_to(scale_ref[i, pl.ds(d, 1), :], (groups, columns))
            out_ref[0, chosen.index(d), i] = corr.astype(jnp.bfloat16)

    pair = [(r, d) for r in range(2) for d in chosen]

    def step(half, carry):
        for b in range(0, len(pair), BLOCK):
            cells_of([(2 * half + r, d) for r, d in pair[b : b + BLOCK]])
        return carry

    lax.fori_loop(0, rows // 2, step, 0)


def costs(slots, warp, tiles, near, far, groups, chosen):
    rows, views, sources, planes, columns = warp.shape
    channels = tiles.shape[1]
    count = len(chosen)
    work = count * views * rows * sources * columns
    return pl.pallas_call(
        functools.partial(cost_kernel, chosen=chosen),
        grid_spec=pltpu.PrefetchScalarGridSpec(
            num_scalar_prefetch=1,
            grid=(views,),
            in_specs=[
                pl.BlockSpec((rows, 1, sources, planes, columns), lambda v, s: (0, v, 0, 0, 0)),
                pl.BlockSpec((1, channels, tiles.shape[2]), lambda v, s: (v, 0, 0)),
                pl.BlockSpec(near.shape, lambda v, s: (0, 0, 0), pipeline_mode=pl.Buffered(1)),
                pl.BlockSpec(far.shape, lambda v, s: (0, 0, 0), pipeline_mode=pl.Buffered(1)),
            ],
            out_specs=pl.BlockSpec((1, count, rows, groups, columns), lambda v, s: (v, 0, 0, 0, 0)),
            scratch_shapes=[
                pltpu.VMEM((sources, rows, planes, columns), jnp.float32),
                pltpu.VMEM((sources, rows, planes, columns), jnp.int32),
                pltpu.VMEM((rows, planes, columns), jnp.float32),
                pltpu.VMEM((BLOCK, channels, columns), jnp.float32),
            ],
        ),
        out_shape=jax.ShapeDtypeStruct((views, count, rows, groups, columns), jnp.bfloat16),
        cost_estimate=pl.CostEstimate(flops=work * 2 * 128 * LOW, bytes_accessed=near.size * 4, transcendentals=0),
        name="cost",
    )(slots, warp, tiles, near, far)


def mix_kernel(weight_ref, before_ref, edge_ref, inner_ref, after_ref, out_ref, rows_ref):
    _, inside, rows, groups, columns = inner_ref.shape
    padded = inside + 4
    lane = lax.broadcasted_iota(jnp.int32, (groups, columns), 1)
    blank = jnp.zeros((groups, columns), jnp.float32)
    empty = jnp.zeros((4 * groups, columns), jnp.bfloat16)
    weight = weight_ref[...]
    terms = []
    for d in range(padded):
        taps = []
        for i in range(rows):
            if d == 0:
                cell = before_ref[0, 0, i]
            elif d == padded - 1:
                cell = after_ref[0, 0, i]
            elif d == 1:
                cell = edge_ref[0, 0, i]
            elif d == padded - 2:
                cell = edge_ref[0, 1, i]
            else:
                cell = inner_ref[0, d - 2, i]
            cell = cell.astype(jnp.float32)
            left = jnp.where(lane == 0, 0.0, pltpu.roll(cell, 1, 1))
            right = jnp.where(lane == columns - 1, 0.0, pltpu.roll(cell, columns - 1, 1))
            taps.append(jnp.concatenate([left, cell, right, blank], axis=0).astype(jnp.bfloat16))
        above = jnp.concatenate([empty] + taps[:-1], axis=1)
        below = jnp.concatenate(taps[1:] + [empty], axis=1)
        matrix = jnp.concatenate([above, jnp.concatenate(taps, axis=1), below], axis=0)
        terms.append(jnp.dot(weight, matrix, preferred_element_type=jnp.float32))
        if d >= 2:
            mixed = terms[d - 2][0:groups] + terms[d - 1][groups : 2 * groups] + terms[d][2 * groups : 3 * groups]
            for i in range(rows):
                rows_ref[pl.ds(i, groups, stride=rows), :] = mixed[:, i * columns : (i + 1) * columns]
            for h in range(groups):
                out_ref[0, h, d - 2] = rows_ref[h * rows : (h + 1) * rows, :].astype(jnp.bfloat16)


def mixed(weight, before, edge, inner, after):
    views, inside, rows, groups, columns = inner.shape

    def part(planes):
        return pl.BlockSpec((1, planes, rows, groups, columns), lambda v: (v, 0, 0, 0, 0))

    return pl.pallas_call(
        mix_kernel,
        grid=(views,),
        in_specs=[pl.BlockSpec(weight.shape, lambda v: (0, 0)), part(1), part(2), part(inside), part(1)],
        out_specs=pl.BlockSpec((1, groups, inside + 2, rows, columns), lambda v: (v, 0, 0, 0, 0)),
        out_shape=jax.ShapeDtypeStruct((views, groups, inside + 2, rows, columns), jnp.bfloat16),
        scratch_shapes=[pltpu.VMEM((groups * rows, columns), jnp.float32)],
        name="mix",
    )(weight, before, edge, inner, after)


def on_device(features, view_lists, requests, warp_idx, conv_weight):
    slabs = lax.axis_size("depth")
    groups = conv_weight.shape[1]
    tiles = jnp.transpose(features, (0, 2, 1))
    channels = tiles.shape[1]
    half = tiles.shape[2] // 2
    send = asked_tiles(jnp.transpose(requests, (0, 2, 1)), tiles)
    near = lax.all_to_all(send, "view", split_axis=0, concat_axis=0, tiled=True)
    near = near.reshape(-1, channels, half)
    far = lax.ppermute(near, "depth", [(i, i ^ 1) for i in range(slabs)])
    warp = packed_warp(warp_idx.reshape(warp_idx.shape[:3] + warp_idx.shape[4:]), slabs)
    warp = lax.all_to_all(warp, "depth", split_axis=0, concat_axis=0, tiled=True)
    planes = warp.shape[3]
    edge = costs(view_lists, warp, tiles, near, far, groups, (0, planes - 1))
    before = lax.ppermute(edge[:, 1:], "depth", [(i, i + 1) for i in range(slabs - 1)])
    after = lax.ppermute(edge[:, :1], "depth", [(i + 1, i) for i in range(slabs - 1)])
    inner = costs(view_lists, warp, tiles, near, far, groups, tuple(range(1, planes - 1)))
    taps = conv_weight.reshape(3, 3, 3 * groups, groups)
    taps = jnp.pad(taps, ((0, 0), (0, 0), (0, groups), (0, 0)))
    weight = jnp.transpose(taps, (0, 3, 1, 2)).reshape(3 * groups, 12 * groups)
    return mixed(weight, before, edge, inner, after)


def solution(mesh):
    return jax.shard_map(
        on_device,
        mesh=mesh,
        in_specs=(
            P("view", None, None),
            P("view", None),
            P(),
            P("view", None, None, "depth", None),
            P(),
        ),
        out_specs=P("view", None, "depth", None, None),
        check_vma=False,
    )
```

```python
import jax
import jax.numpy as jnp
from jax import lax
from jax.experimental import pallas as pl
from jax.experimental.pallas import tpu as pltpu
from jax.sharding import PartitionSpec as P

LOW = 256
F8 = jnp.float8_e4m3fn


def ask_kernel(requests_ref, tiles_ref, out_ref):
    here = lax.axis_index("view")
    half = out_ref.shape[3]
    start = pl.multiple_of((lax.axis_index("depth") % 2) * half, half)
    for u in range(out_ref.shape[0]):
        for c in range(out_ref.shape[1]):
            out_ref[u, c] = tiles_ref[requests_ref[u, c, here], :, pl.ds(start, half)]


def asked_tiles(requests, tiles):
    askers, slots, _ = requests.shape
    _, channels, pixels = tiles.shape
    return pl.pallas_call(
        ask_kernel,
        in_specs=[pl.BlockSpec(memory_space=pltpu.SMEM), pl.BlockSpec(memory_space=pltpu.VMEM)],
        out_specs=pl.BlockSpec(memory_space=pltpu.VMEM),
        out_shape=jax.ShapeDtypeStruct((askers, slots, channels, pixels // 2), jnp.bfloat16),
        compiler_params=pltpu.CompilerParams(vmem_limit_bytes=8 << 20),
        name="ask",
    )(requests, tiles)


def pack_kernel(warp_ref, *refs):
    *out_refs, rows_ref = refs
    views, sources, planes, _ = warp_ref.shape
    slabs = len(out_refs)
    slab = planes // slabs
    here = lax.axis_index("depth")
    for k, out_ref in enumerate(out_refs):
        t = (here + k) % slabs
        first = pl.multiple_of(t * slab, slab)
        before = jnp.maximum(first - 1, 0)
        after = jnp.minimum(first + slab, planes - 1)
        for v in range(views):
            for s in range(sources):
                r = s * (slab + 2)
                rows_ref[r + 1 : r + 1 + slab] = warp_ref[v, s, pl.ds(first, slab), :]
                rows_ref[r : r + 1] = jnp.where(t == 0, -1, warp_ref[v, s, pl.ds(before, 1), :])
                rows_ref[r + 1 + slab : r + 2 + slab] = jnp.where(
                    t == slabs - 1, -1, warp_ref[v, s, pl.ds(after, 1), :]
                )
            out_ref[v] = rows_ref[...].astype(jnp.int16)


def packed_warp(warp, slabs):
    views, sources, planes, columns = warp.shape
    rows = sources * (planes // slabs + 2)
    return pl.pallas_call(
        pack_kernel,
        in_specs=[pl.BlockSpec(memory_space=pltpu.VMEM)],
        out_specs=[pl.BlockSpec(memory_space=pltpu.VMEM)] * slabs,
        out_shape=[jax.ShapeDtypeStruct((views, rows, columns), jnp.int16)] * slabs,
        scratch_shapes=[pltpu.VMEM((rows, columns), jnp.int32)],
        cost_estimate=pl.CostEstimate(flops=warp.size, bytes_accessed=warp.size * 6, transcendentals=0),
        compiler_params=pltpu.CompilerParams(vmem_limit_bytes=8 << 20),
        name="pack",
    )(warp)


def cost_mix_kernel(slot_ref, *refs):
    warp_refs = refs[:-13]
    own_ref, near_ref, far_ref, weight_ref, out_ref = refs[-13:-8]
    parts_ref, unit_ref, low_ref, high_ref, scale_ref, sums_ref, taps_ref, rows_ref = refs[-8:]
    view = pl.program_id(0)
    rows = len(warp_refs)
    columns = warp_refs[0].shape[2]
    sources = slot_ref.shape[1]
    planes = warp_refs[0].shape[1] // sources
    channels = own_ref.shape[1]
    groups = out_ref.shape[1]
    size = channels // groups
    here = lax.axis_index("depth")
    flip = (here % 2) * 2

    @pl.when(view == 0)
    def _():
        most = jnp.zeros(near_ref.shape[1:], jnp.bfloat16)
        for slot in range(near_ref.shape[0]):
            most = jnp.maximum(most, jnp.maximum(jnp.abs(near_ref[slot]), jnp.abs(far_ref[slot])))
        peak = jnp.max(most.astype(jnp.float32))
        unit = jnp.float32(1.0)
        for power in (32, 16, 8, 4, 2, 1):
            grown = unit * jnp.float32(2.0**power)
            unit = jnp.where(peak * grown <= 256.0, grown, unit)
        unit_ref[0] = 1.0 / unit
        unit = unit.astype(jnp.bfloat16)

        def split(slot, carry):
            for h in range(4):
                ref = near_ref if h < 2 else far_ref
                value = ref[slot, :, (h % 2) * LOW : (h % 2 + 1) * LOW] * unit
                coarse = value.astype(F8)
                parts_ref[slot, h * channels : (h + 1) * channels] = coarse
                parts_ref[slot, (4 + h) * channels : (5 + h) * channels] = (value - coarse.astype(jnp.bfloat16)).astype(F8)
            return carry

        lax.fori_loop(0, near_ref.shape[0], split, 0)

    for k in range(rows):
        i = (here + rows - k) % rows
        warp = warp_refs[k][0].astype(jnp.int32)
        outside = warp < 0
        low_ref[i] = jnp.where(outside, -1, warp & (LOW - 1)).astype(jnp.float32)
        high_ref[i] = (warp >> 8) ^ flip
        sums_ref[0 : sources * planes] = jnp.where(outside, 0.0, 1.0)
        live = sums_ref[0:planes]
        for s in range(1, sources):
            live = live + sums_ref[s * planes : (s + 1) * planes]
        scale_ref[i] = (0.5 * unit_ref[0]) / jnp.maximum(live, 1.0)

    tiles = LOW // 16
    pixel = lax.broadcasted_iota(jnp.int32, (tiles, 16, columns), 0) * 16 + lax.broadcasted_iota(
        jnp.int32, (tiles, 16, columns), 1
    )
    pixel = pixel.astype(jnp.float32).astype(jnp.bfloat16)
    one = jnp.ones((), jnp.bfloat16)
    zero = jnp.zeros((), jnp.bfloat16)
    lane = lax.broadcasted_iota(jnp.int32, (groups, columns), 1)
    blank = jnp.zeros((groups, columns), jnp.float32)

    def plane(d, carry):
        totals = [jnp.zeros((channels, columns), jnp.float32) for _ in range(rows)]
        for s in range(sources):
            lhs = parts_ref[slot_ref[view, s]]
            hots = []
            for i in range(rows):
                row = jnp.broadcast_to(low_ref[i, pl.ds(s * planes + d, 1), :], (16, columns)).astype(jnp.bfloat16)
                hots.append(jnp.where(pixel == row[None], one, zero).reshape(LOW, columns).astype(F8))
            picked = jnp.dot(lhs, jnp.concatenate(hots, axis=1), preferred_element_type=jnp.float32)
            for i in range(rows):
                high = jnp.broadcast_to(high_ref[i, pl.ds(s * planes + d, 1), :], (channels, columns))
                odd = (high & 1) == 1
                upper = (high & 2) == 2
                part = picked[:, i * columns : (i + 1) * columns]
                part = part[: 4 * channels] + part[4 * channels :]
                q = [part[h * channels : (h + 1) * channels] for h in range(4)]
                totals[i] = totals[i] + jnp.where(upper, jnp.where(odd, q[3], q[2]), jnp.where(odd, q[1], q[0]))
        for i in range(rows):
            own = own_ref[0, :, i * columns : (i + 1) * columns].astype(jnp.float32)
            start = i * channels
            sums_ref[start : start + channels] = totals[i] * own
            corr = sums_ref[pl.ds(start, groups, stride=size), :]
            for n in range(1, size):
                corr = corr + sums_ref[pl.ds(start + n, groups, stride=size), :]
            cell = corr * jnp.broadcast_to(scale_ref[i, pl.ds(d, 1), :], (groups, columns))
            left = jnp.where(lane == 0, 0.0, pltpu.roll(cell, 1, 1))
            right = jnp.where(lane == columns - 1, 0.0, pltpu.roll(cell, columns - 1, 1))
            taps_ref[d, i] = jnp.concatenate([left, cell, right, blank], axis=0).astype(jnp.bfloat16)
        return carry

    lax.fori_loop(0, planes, plane, 0)

    empty = jnp.zeros((4 * groups, columns), jnp.bfloat16)
    weight = weight_ref[...]
    terms = []
    for d in range(planes):
        taps = [taps_ref[d, i] for i in range(rows)]
        above = jnp.concatenate([empty] + taps[:-1], axis=1)
        below = jnp.concatenate(taps[1:] + [empty], axis=1)
        matrix = jnp.concatenate([above, jnp.concatenate(taps, axis=1), below], axis=0)
        terms.append(jnp.dot(weight, matrix, preferred_element_type=jnp.float32))
        if d >= 2:
            mixed = terms[d - 2][0:groups] + terms[d - 1][groups : 2 * groups] + terms[d][2 * groups : 3 * groups]
            for i in range(rows):
                rows_ref[pl.ds(i, groups, stride=rows), :] = mixed[:, i * columns : (i + 1) * columns]
            for h in range(groups):
                out_ref[0, h, d - 2] = rows_ref[h * rows : (h + 1) * rows, :].astype(jnp.bfloat16)


def cost_mix(slots, warps, tiles, near, far, weight, groups):
    rows = len(warps)
    views, sources = slots.shape
    columns = warps[0].shape[2]
    planes = warps[0].shape[1] // sources
    channels = tiles.shape[1]
    whole = {"pipeline_mode": pl.Buffered(1)}
    return pl.pallas_call(
        cost_mix_kernel,
        grid_spec=pltpu.PrefetchScalarGridSpec(
            num_scalar_prefetch=1,
            grid=(views,),
            in_specs=[pl.BlockSpec((1, sources * planes, columns), lambda v, s: (v, 0, 0))] * rows
            + [
                pl.BlockSpec((1, channels, tiles.shape[2]), lambda v, s: (v, 0, 0)),
                pl.BlockSpec(near.shape, lambda v, s: (0, 0, 0), **whole),
                pl.BlockSpec(far.shape, lambda v, s: (0, 0, 0), **whole),
                pl.BlockSpec(weight.shape, lambda v, s: (0, 0), **whole),
            ],
            out_specs=pl.BlockSpec((1, groups, planes - 2, rows, columns), lambda v, s: (v, 0, 0, 0, 0)),
            scratch_shapes=[
                pltpu.VMEM((near.shape[0], 8 * channels, LOW), F8),
                pltpu.SMEM((1,), jnp.float32),
                pltpu.VMEM((rows, sources * planes, columns), jnp.float32),
                pltpu.VMEM((rows, sources * planes, columns), jnp.int32),
                pltpu.VMEM((rows, planes, columns), jnp.float32),
                pltpu.VMEM((rows * channels, columns), jnp.float32),
                pltpu.VMEM((planes, rows, 4 * groups, columns), jnp.bfloat16),
                pltpu.VMEM((groups * rows, columns), jnp.float32),
            ],
        ),
        out_shape=jax.ShapeDtypeStruct((views, groups, planes - 2, rows, columns), jnp.bfloat16),
        compiler_params=pltpu.CompilerParams(vmem_limit_bytes=24 << 20),
        name="costmix",
    )(slots, *warps, tiles, near, far, weight)


def on_device(features, view_lists, requests, warp_idx, conv_weight):
    slabs = lax.axis_size("depth")
    groups = conv_weight.shape[1]
    tiles = jnp.transpose(features, (0, 2, 1))
    channels = tiles.shape[1]
    half = tiles.shape[2] // 2
    send = asked_tiles(jnp.transpose(requests, (0, 2, 1)), tiles)
    near = lax.all_to_all(send, "view", split_axis=0, concat_axis=0, tiled=True)
    near = near.reshape(-1, channels, half)
    warps = packed_warp(warp_idx.reshape(warp_idx.shape[:3] + warp_idx.shape[4:]), slabs)
    warps = [warps[0]] + [
        lax.ppermute(warps[k], "depth", [(i, (i + k) % slabs) for i in range(slabs)]) for k in range(1, slabs)
    ]
    near, *warps = lax.optimization_barrier((near, *warps))
    far = lax.ppermute(near, "depth", [(i, i ^ 1) for i in range(slabs)])
    taps = conv_weight.reshape(3, 3, 3 * groups, groups)
    taps = jnp.pad(taps, ((0, 0), (0, 0), (0, groups), (0, 0)))
    weight = jnp.transpose(taps, (0, 3, 1, 2)).reshape(3 * groups, 12 * groups)
    return cost_mix(view_lists, warps, tiles, near, far, weight, groups)


def solution(mesh):
    return jax.shard_map(
        on_device,
        mesh=mesh,
        in_specs=(
            P("view", None, None),
            P("view", None),
            P(),
            P("view", None, None, "depth", None),
            P(),
        ),
        out_specs=P("view", None, "depth", None, None),
        check_vma=False,
    )
```

```python
import jax
import jax.numpy as jnp
from jax import lax
from jax.experimental import pallas as pl
from jax.experimental.pallas import tpu as pltpu
from jax.sharding import PartitionSpec as P

LOW = 256


def ask_kernel(requests_ref, tiles_ref, out_ref):
    here = lax.axis_index("view")
    count, slots, _, half = out_ref.shape
    first = pl.program_id(0) * count
    start = pl.multiple_of((lax.axis_index("depth") % 2) * half, half)
    for u in range(count):
        for c in range(slots):
            out_ref[u, c] = tiles_ref[requests_ref[first + u, c, here], :, pl.ds(start, half)]


def asked_tiles(requests, tiles):
    askers, slots, _ = requests.shape
    _, channels, pixels = tiles.shape
    return pl.pallas_call(
        ask_kernel,
        grid=(4,),
        in_specs=[
            pl.BlockSpec(memory_space=pltpu.SMEM),
            pl.BlockSpec(tiles.shape, lambda n: (0, 0, 0), pipeline_mode=pl.Buffered(1)),
        ],
        out_specs=pl.BlockSpec((askers // 4, slots, channels, pixels // 2), lambda n: (n, 0, 0, 0)),
        out_shape=jax.ShapeDtypeStruct((askers, slots, channels, pixels // 2), jnp.bfloat16),
        name="ask",
    )(requests, tiles)


def pack_kernel(warp_ref, *refs):
    *out_refs, rows_ref = refs
    views, sources, planes, _ = warp_ref.shape
    slabs = len(out_refs)
    slab = planes // slabs
    here = lax.axis_index("depth")
    for k, out_ref in enumerate(out_refs):
        t = (here + k) % slabs
        first = pl.multiple_of(t * slab, slab)
        before = jnp.maximum(first - 1, 0)
        after = jnp.minimum(first + slab, planes - 1)
        for v in range(views):
            for s in range(sources):
                r = s * (slab + 2)
                rows_ref[r + 1 : r + 1 + slab] = warp_ref[v, s, pl.ds(first, slab), :]
                rows_ref[r : r + 1] = jnp.where(t == 0, -1, warp_ref[v, s, pl.ds(before, 1), :])
                rows_ref[r + 1 + slab : r + 2 + slab] = jnp.where(
                    t == slabs - 1, -1, warp_ref[v, s, pl.ds(after, 1), :]
                )
            out_ref[v] = rows_ref[...].astype(jnp.int16)


def packed_warp(warp, slabs):
    views, sources, planes, columns = warp.shape
    rows = sources * (planes // slabs + 2)
    return pl.pallas_call(
        pack_kernel,
        in_specs=[pl.BlockSpec(memory_space=pltpu.VMEM)],
        out_specs=[pl.BlockSpec(memory_space=pltpu.VMEM)] * slabs,
        out_shape=[jax.ShapeDtypeStruct((views, rows, columns), jnp.int16)] * slabs,
        scratch_shapes=[pltpu.VMEM((rows, columns), jnp.int32)],
        cost_estimate=pl.CostEstimate(flops=warp.size, bytes_accessed=warp.size * 6, transcendentals=0),
        compiler_params=pltpu.CompilerParams(vmem_limit_bytes=8 << 20),
        name="pack",
    )(warp)


def cost_mix_kernel(slot_ref, *refs):
    warp_refs = refs[:-11]
    own_ref, near_ref, far_ref, weight_ref, out_ref = refs[-11:-6]
    low_ref, high_ref, scale_ref, sums_ref, taps_ref, rows_ref = refs[-6:]
    view = pl.program_id(0)
    rows = len(warp_refs)
    columns = warp_refs[0].shape[2]
    sources = slot_ref.shape[1]
    planes = warp_refs[0].shape[1] // sources
    channels = own_ref.shape[1]
    groups = out_ref.shape[1]
    size = channels // groups
    here = lax.axis_index("depth")
    flip = (here % 2) * 2

    for k in range(rows):
        i = (here + rows - k) % rows
        warp = warp_refs[k][0].astype(jnp.int32)
        outside = warp < 0
        low_ref[i] = jnp.where(outside, -1, warp & (LOW - 1)).astype(jnp.float32)
        high_ref[i] = (warp >> 8) ^ flip
        sums_ref[0 : sources * planes] = jnp.where(outside, 0.0, 1.0)
        live = sums_ref[0:planes]
        for s in range(1, sources):
            live = live + sums_ref[s * planes : (s + 1) * planes]
        scale_ref[i] = 0.5 / jnp.maximum(live, 1.0)

    tiles = LOW // 16
    pixel = lax.broadcasted_iota(jnp.int32, (tiles, 16, columns), 0) * 16 + lax.broadcasted_iota(
        jnp.int32, (tiles, 16, columns), 1
    )
    pixel = pixel.astype(jnp.float32).astype(jnp.bfloat16)
    one = jnp.ones((), jnp.bfloat16)
    zero = jnp.zeros((), jnp.bfloat16)
    lane = lax.broadcasted_iota(jnp.int32, (groups, columns), 1)
    blank = jnp.zeros((groups, columns), jnp.float32)

    def plane(d, carry):
        totals = [jnp.zeros((channels, columns), jnp.float32) for _ in range(rows)]
        for s in range(sources):
            near = near_ref[slot_ref[view, s]]
            far = far_ref[slot_ref[view, s]]
            lhs = jnp.concatenate([near[:, :LOW], near[:, LOW:], far[:, :LOW], far[:, LOW:]], axis=0)
            hots = []
            for i in range(rows):
                row = jnp.broadcast_to(low_ref[i, pl.ds(s * planes + d, 1), :], (16, columns)).astype(jnp.bfloat16)
                hots.append(jnp.where(pixel == row[None], one, zero).reshape(LOW, columns))
            picked = jnp.dot(lhs, jnp.concatenate(hots, axis=1), preferred_element_type=jnp.float32)
            for i in range(rows):
                high = jnp.broadcast_to(high_ref[i, pl.ds(s * planes + d, 1), :], (channels, columns))
                odd = (high & 1) == 1
                upper = (high & 2) == 2
                part = picked[:, i * columns : (i + 1) * columns]
                q = [part[h * channels : (h + 1) * channels] for h in range(4)]
                totals[i] = totals[i] + jnp.where(upper, jnp.where(odd, q[3], q[2]), jnp.where(odd, q[1], q[0]))
        for i in range(rows):
            own = own_ref[0, :, i * columns : (i + 1) * columns].astype(jnp.float32)
            start = i * channels
            sums_ref[start : start + channels] = totals[i] * own
            corr = sums_ref[pl.ds(start, groups, stride=size), :]
            for n in range(1, size):
                corr = corr + sums_ref[pl.ds(start + n, groups, stride=size), :]
            cell = corr * jnp.broadcast_to(scale_ref[i, pl.ds(d, 1), :], (groups, columns))
            left = jnp.where(lane == 0, 0.0, pltpu.roll(cell, 1, 1))
            right = jnp.where(lane == columns - 1, 0.0, pltpu.roll(cell, columns - 1, 1))
            taps_ref[d, i] = jnp.concatenate([left, cell, right, blank], axis=0).astype(jnp.bfloat16)
        return carry

    lax.fori_loop(0, planes, plane, 0, unroll=5)

    empty = jnp.zeros((4 * groups, columns), jnp.bfloat16)
    weight = weight_ref[...]
    terms = []
    for d in range(planes):
        taps = [taps_ref[d, i] for i in range(rows)]
        above = jnp.concatenate([empty] + taps[:-1], axis=1)
        below = jnp.concatenate(taps[1:] + [empty], axis=1)
        matrix = jnp.concatenate([above, jnp.concatenate(taps, axis=1), below], axis=0)
        terms.append(jnp.dot(weight, matrix, preferred_element_type=jnp.float32))
        if d >= 2:
            mixed = terms[d - 2][0:groups] + terms[d - 1][groups : 2 * groups] + terms[d][2 * groups : 3 * groups]
            for i in range(rows):
                rows_ref[pl.ds(i, groups, stride=rows), :] = mixed[:, i * columns : (i + 1) * columns]
            for h in range(groups):
                out_ref[0, h, d - 2] = rows_ref[h * rows : (h + 1) * rows, :].astype(jnp.bfloat16)


def cost_mix(slots, warps, tiles, near, far, weight, groups):
    rows = len(warps)
    views, sources = slots.shape
    columns = warps[0].shape[2]
    planes = warps[0].shape[1] // sources
    channels = tiles.shape[1]
    whole = {"pipeline_mode": pl.Buffered(1)}
    return pl.pallas_call(
        cost_mix_kernel,
        grid_spec=pltpu.PrefetchScalarGridSpec(
            num_scalar_prefetch=1,
            grid=(views,),
            in_specs=[pl.BlockSpec((1, sources * planes, columns), lambda v, s: (v, 0, 0))] * rows
            + [
                pl.BlockSpec((1, channels, tiles.shape[2]), lambda v, s: (v, 0, 0)),
                pl.BlockSpec(near.shape, lambda v, s: (0, 0, 0), **whole),
                pl.BlockSpec(far.shape, lambda v, s: (0, 0, 0), **whole),
                pl.BlockSpec(weight.shape, lambda v, s: (0, 0), **whole),
            ],
            out_specs=pl.BlockSpec((1, groups, planes - 2, rows, columns), lambda v, s: (v, 0, 0, 0, 0)),
            scratch_shapes=[
                pltpu.VMEM((rows, sources * planes, columns), jnp.float32),
                pltpu.VMEM((rows, sources * planes, columns), jnp.int32),
                pltpu.VMEM((rows, planes, columns), jnp.float32),
                pltpu.VMEM((rows * channels, columns), jnp.float32),
                pltpu.VMEM((planes, rows, 4 * groups, columns), jnp.bfloat16),
                pltpu.VMEM((groups * rows, columns), jnp.float32),
            ],
        ),
        out_shape=jax.ShapeDtypeStruct((views, groups, planes - 2, rows, columns), jnp.bfloat16),
        compiler_params=pltpu.CompilerParams(vmem_limit_bytes=24 << 20),
        name="costmix",
    )(slots, *warps, tiles, near, far, weight)


def on_device(features, view_lists, requests, warp_idx, conv_weight):
    slabs = lax.axis_size("depth")
    groups = conv_weight.shape[1]
    tiles = jnp.transpose(features, (0, 2, 1))
    channels = tiles.shape[1]
    half = tiles.shape[2] // 2
    send = asked_tiles(jnp.transpose(requests, (0, 2, 1)), tiles)
    near = lax.all_to_all(send, "view", split_axis=0, concat_axis=0, tiled=True)
    near = near.reshape(-1, channels, half)
    warps = packed_warp(warp_idx.reshape(warp_idx.shape[:3] + warp_idx.shape[4:]), slabs)
    warps = [warps[0]] + [
        lax.ppermute(warps[k], "depth", [(i, (i + k) % slabs) for i in range(slabs)]) for k in range(1, slabs)
    ]
    near, *warps = lax.optimization_barrier((near, *warps))
    far = lax.ppermute(near, "depth", [(i, i ^ 1) for i in range(slabs)])
    taps = conv_weight.reshape(3, 3, 3 * groups, groups)
    taps = jnp.pad(taps, ((0, 0), (0, 0), (0, groups), (0, 0)))
    weight = jnp.transpose(taps, (0, 3, 1, 2)).reshape(3 * groups, 12 * groups)
    return cost_mix(view_lists, warps, tiles, near, far, weight, groups)


def solution(mesh):
    return jax.shard_map(
        on_device,
        mesh=mesh,
        in_specs=(
            P("view", None, None),
            P("view", None),
            P(),
            P("view", None, None, "depth", None),
            P(),
        ),
        out_specs=P("view", None, "depth", None, None),
        check_vma=False,
    )
```

```python
import jax
import jax.numpy as jnp
from jax import lax
from jax.experimental import pallas as pl
from jax.experimental.pallas import tpu as pltpu
from jax.sharding import PartitionSpec as P

LOW = 256
GATHERED = 2


def ask_kernel(requests_ref, tiles_ref, out_ref):
    here = lax.axis_index("view")
    count, slots, _, half = out_ref.shape
    start = pl.multiple_of((lax.axis_index("depth") % 2) * half, half)
    for u in range(count):
        for c in range(slots):
            out_ref[u, c] = tiles_ref[requests_ref[u, c, here], :, pl.ds(start, half)]


def asked_tiles(requests, tiles):
    askers, slots, _ = requests.shape
    _, channels, pixels = tiles.shape
    return pl.pallas_call(
        ask_kernel,
        in_specs=[pl.BlockSpec(memory_space=pltpu.SMEM), pl.BlockSpec(memory_space=pltpu.VMEM)],
        out_specs=pl.BlockSpec(memory_space=pltpu.VMEM),
        out_shape=jax.ShapeDtypeStruct((askers, slots, channels, pixels // 2), jnp.bfloat16),
        name="ask",
    )(requests, tiles)


def pack_kernel(warp_ref, *refs):
    *out_refs, rows_ref = refs
    views, sources, planes, _ = warp_ref.shape
    slabs = len(out_refs)
    slab = planes // slabs
    here = lax.axis_index("depth")
    for k, out_ref in enumerate(out_refs):
        t = (here + k) % slabs
        first = pl.multiple_of(t * slab, slab)
        before = jnp.maximum(first - 1, 0)
        after = jnp.minimum(first + slab, planes - 1)
        for v in range(views):
            for s in range(sources):
                r = s * (slab + 2)
                rows_ref[r + 1 : r + 1 + slab] = warp_ref[v, s, pl.ds(first, slab), :]
                rows_ref[r : r + 1] = jnp.where(t == 0, -1, warp_ref[v, s, pl.ds(before, 1), :])
                rows_ref[r + 1 + slab : r + 2 + slab] = jnp.where(
                    t == slabs - 1, -1, warp_ref[v, s, pl.ds(after, 1), :]
                )
            out_ref[v] = rows_ref[...].astype(jnp.int16)


def packed_warp(warp, slabs):
    views, sources, planes, columns = warp.shape
    rows = sources * (planes // slabs + 2)
    return pl.pallas_call(
        pack_kernel,
        in_specs=[pl.BlockSpec(memory_space=pltpu.VMEM)],
        out_specs=[pl.BlockSpec(memory_space=pltpu.VMEM)] * slabs,
        out_shape=[jax.ShapeDtypeStruct((views, rows, columns), jnp.int16)] * slabs,
        scratch_shapes=[pltpu.VMEM((rows, columns), jnp.int32)],
        cost_estimate=pl.CostEstimate(flops=warp.size, bytes_accessed=warp.size * 6, transcendentals=0),
        compiler_params=pltpu.CompilerParams(vmem_limit_bytes=8 << 20),
        name="pack",
    )(warp)


def lanes_at(table, lanes):
    numbers = lax.GatherDimensionNumbers(
        offset_dims=(),
        collapsed_slice_dims=(1,),
        start_index_map=(1,),
        operand_batching_dims=(0,),
        start_indices_batching_dims=(0,),
    )
    return lax.gather(table, lanes[..., None], numbers, (1, 1), mode=lax.GatherScatterMode.PROMISE_IN_BOUNDS)


def cost_mix_kernel(slot_ref, *refs):
    warp_refs = refs[:-15]
    own_ref, near_ref, far_ref, weight_ref, out_ref = refs[-15:-10]
    low_ref, high_ref, scale_ref, sums_ref, taps_ref, rows_ref, table_ref, pick_ref, extra_ref, mine_ref = refs[-10:]
    view = pl.program_id(0)
    rows = len(warp_refs)
    columns = warp_refs[0].shape[2]
    sources = slot_ref.shape[1]
    planes = warp_refs[0].shape[1] // sources
    channels = own_ref.shape[1]
    groups = out_ref.shape[1]
    size = channels // groups
    half = near_ref.shape[2]
    gathered = table_ref.shape[0]
    dotted = sources - gathered
    here = lax.axis_index("depth")
    flip = (here % 2) * 2

    for k in range(rows):
        i = (here + rows - k) % rows
        warp = warp_refs[k][0].astype(jnp.int32)
        outside = warp < 0
        low_ref[i] = jnp.where(outside, -1, warp & (LOW - 1)).astype(jnp.float32)
        high_ref[i] = (warp >> 8) ^ flip
        sums_ref[0 : sources * planes] = jnp.where(outside, 0.0, 1.0)
        live = sums_ref[0:planes]
        for s in range(1, sources):
            live = live + sums_ref[s * planes : (s + 1) * planes]
        scale_ref[i] = 0.5 / jnp.maximum(live, 1.0)
        for x in range(gathered):
            picks = warp[(dotted + x) * planes : (dotted + x + 1) * planes]
            pick_ref[x, pl.ds(i, planes, stride=rows), :] = picks
    for x in range(gathered):
        slot = slot_ref[view, dotted + x]
        table_ref[x, :, :half] = near_ref[slot].astype(jnp.float32)
        table_ref[x, :, half:] = far_ref[slot].astype(jnp.float32)
    for i in range(rows):
        extra_ref[0:channels] = own_ref[0, :, i * columns : (i + 1) * columns].astype(jnp.float32)
        for n in range(size):
            mine_ref[i, n] = extra_ref[pl.ds(n, groups, stride=size), :]

    tiles = LOW // 16
    pixel = lax.broadcasted_iota(jnp.int32, (tiles, 16, columns), 0) * 16 + lax.broadcasted_iota(
        jnp.int32, (tiles, 16, columns), 1
    )
    pixel = pixel.astype(jnp.float32).astype(jnp.bfloat16)
    one = jnp.ones((), jnp.bfloat16)
    zero = jnp.zeros((), jnp.bfloat16)
    lane = lax.broadcasted_iota(jnp.int32, (groups, columns), 1)
    blank = jnp.zeros((groups, columns), jnp.float32)

    def dot_source(totals, s, d):
        near = near_ref[slot_ref[view, s]]
        far = far_ref[slot_ref[view, s]]
        lhs = jnp.concatenate([near[:, :LOW], near[:, LOW:], far[:, :LOW], far[:, LOW:]], axis=0)
        hots = []
        for i in range(rows):
            row = jnp.broadcast_to(low_ref[i, pl.ds(s * planes + d, 1), :], (16, columns)).astype(jnp.bfloat16)
            hots.append(jnp.where(pixel == row[None], one, zero).reshape(LOW, columns))
        picked = jnp.dot(lhs, jnp.concatenate(hots, axis=1), preferred_element_type=jnp.float32)
        for i in range(rows):
            high = jnp.broadcast_to(high_ref[i, pl.ds(s * planes + d, 1), :], (channels, columns))
            odd = (high & 1) == 1
            upper = (high & 2) == 2
            part = picked[:, i * columns : (i + 1) * columns]
            q = [part[h * channels : (h + 1) * channels] for h in range(4)]
            totals[i] = totals[i] + jnp.where(upper, jnp.where(odd, q[3], q[2]), jnp.where(odd, q[1], q[0]))

    def gather_masks(x, d):
        picks = pick_ref[x, d * rows : (d + 2) * rows]
        outside = picks < 0
        block = (picks >> 7) ^ (flip * 2)

        def bit(value):
            return value.astype(jnp.float32).astype(jnp.bfloat16) > 0.5

        bits = [bit(block & 1), bit(block & 2), bit(block & 4)]
        return (picks & (columns - 1)).astype(jnp.int16), bits, bit(jnp.where(outside, 0, 1))

    def gather_channel(n, masks):
        total = jnp.zeros((2 * rows, columns), jnp.float32)
        for x in range(gathered):
            lanes, bits, inside = masks[x]
            found = []
            for h in range(8):
                row = table_ref[x, n : n + 1, h * columns : (h + 1) * columns]
                found.append(lanes_at(jnp.broadcast_to(row, (2 * rows, columns)).astype(jnp.bfloat16), lanes))
            for mask in bits:
                found = [jnp.where(mask, found[j + 1], found[j]) for j in range(0, len(found), 2)]
            total = total + jnp.where(inside, found[0], zero).astype(jnp.float32)
        return total

    for d in range(0, planes, 2):
        side = (d // 2) % 2
        base = side * 2 * rows * channels
        masks = [gather_masks(x, d) for x in range(gathered)]
        share = -(-channels // (2 * dotted))
        done = 0
        for p in range(2):
            totals = [jnp.zeros((channels, columns), jnp.float32) for _ in range(rows)]
            for s in range(dotted):
                dot_source(totals, s, d + p)
                for n in range(done, min(done + share, channels)):
                    total = gather_channel(n, masks)
                    for r in range(2):
                        at = base + (r * channels + n) * rows
                        extra_ref[at : at + rows] = total[r * rows : (r + 1) * rows]
                done = min(done + share, channels)
            for i in range(rows):
                at = base + (p * rows + i) * channels
                sums_ref[at : at + channels] = totals[i]
        for p in range(2):
            for i in range(rows):
                corr = None
                for n in range(size):
                    dots = sums_ref[pl.ds(base + (p * rows + i) * channels + n, groups, stride=size), :]
                    more = extra_ref[pl.ds(base + (p * channels + n) * rows + i, groups, stride=size * rows), :]
                    term = (dots + more) * mine_ref[i, n]
                    corr = term if corr is None else corr + term
                cell = corr * jnp.broadcast_to(scale_ref[i, d + p : d + p + 1, :], (groups, columns))
                left = jnp.where(lane == 0, 0.0, pltpu.roll(cell, 1, 1))
                right = jnp.where(lane == columns - 1, 0.0, pltpu.roll(cell, columns - 1, 1))
                taps_ref[d + p, i] = jnp.concatenate([left, cell, right, blank], axis=0).astype(jnp.bfloat16)

    empty = jnp.zeros((4 * groups, columns), jnp.bfloat16)
    weight = weight_ref[...]
    terms = []
    for d in range(planes):
        taps = [taps_ref[d, i] for i in range(rows)]
        above = jnp.concatenate([empty] + taps[:-1], axis=1)
        below = jnp.concatenate(taps[1:] + [empty], axis=1)
        matrix = jnp.concatenate([above, jnp.concatenate(taps, axis=1), below], axis=0)
        terms.append(jnp.dot(weight, matrix, preferred_element_type=jnp.float32))
        if d >= 2:
            mixed = terms[d - 2][0:groups] + terms[d - 1][groups : 2 * groups] + terms[d][2 * groups : 3 * groups]
            for i in range(rows):
                rows_ref[pl.ds(i, groups, stride=rows), :] = mixed[:, i * columns : (i + 1) * columns]
            for h in range(groups):
                out_ref[0, h, d - 2] = rows_ref[h * rows : (h + 1) * rows, :].astype(jnp.bfloat16)


def cost_mix(slots, warps, tiles, near, far, weight, groups):
    rows = len(warps)
    views, sources = slots.shape
    columns = warps[0].shape[2]
    planes = warps[0].shape[1] // sources
    channels = tiles.shape[1]
    whole = {"pipeline_mode": pl.Buffered(1)}
    return pl.pallas_call(
        cost_mix_kernel,
        grid_spec=pltpu.PrefetchScalarGridSpec(
            num_scalar_prefetch=1,
            grid=(views,),
            in_specs=[pl.BlockSpec((1, sources * planes, columns), lambda v, s: (v, 0, 0))] * rows
            + [
                pl.BlockSpec((1, channels, tiles.shape[2]), lambda v, s: (v, 0, 0)),
                pl.BlockSpec(near.shape, lambda v, s: (0, 0, 0), **whole),
                pl.BlockSpec(far.shape, lambda v, s: (0, 0, 0), **whole),
                pl.BlockSpec(weight.shape, lambda v, s: (0, 0), **whole),
            ],
            out_specs=pl.BlockSpec((1, groups, planes - 2, rows, columns), lambda v, s: (v, 0, 0, 0, 0)),
            scratch_shapes=[
                pltpu.VMEM((rows, sources * planes, columns), jnp.float32),
                pltpu.VMEM((rows, sources * planes, columns), jnp.int32),
                pltpu.VMEM((rows, planes, columns), jnp.float32),
                pltpu.VMEM((4 * rows * channels, columns), jnp.float32),
                pltpu.VMEM((planes, rows, 4 * groups, columns), jnp.bfloat16),
                pltpu.VMEM((groups * rows, columns), jnp.float32),
                pltpu.VMEM((GATHERED, channels, tiles.shape[2]), jnp.float32),
                pltpu.VMEM((GATHERED, planes * rows, columns), jnp.int32),
                pltpu.VMEM((4 * rows * channels, columns), jnp.float32),
                pltpu.VMEM((rows, channels // groups, groups, columns), jnp.float32),
            ],
        ),
        out_shape=jax.ShapeDtypeStruct((views, groups, planes - 2, rows, columns), jnp.bfloat16),
        compiler_params=pltpu.CompilerParams(vmem_limit_bytes=24 << 20),
        name="costmix",
    )(slots, *warps, tiles, near, far, weight)


def on_device(features, view_lists, requests, warp_idx, conv_weight):
    slabs = lax.axis_size("depth")
    groups = conv_weight.shape[1]
    tiles = jnp.transpose(features, (0, 2, 1))
    channels = tiles.shape[1]
    half = tiles.shape[2] // 2
    send = asked_tiles(jnp.transpose(requests, (0, 2, 1)), tiles)
    near = lax.all_to_all(send, "view", split_axis=0, concat_axis=0, tiled=True)
    near = near.reshape(-1, channels, half)
    warps = packed_warp(warp_idx.reshape(warp_idx.shape[:3] + warp_idx.shape[4:]), slabs)
    warps = [warps[0]] + [
        lax.ppermute(warps[k], "depth", [(i, (i + k) % slabs) for i in range(slabs)]) for k in range(1, slabs)
    ]
    near, *warps = lax.optimization_barrier((near, *warps))
    far = lax.ppermute(near, "depth", [(i, i ^ 1) for i in range(slabs)])
    taps = conv_weight.reshape(3, 3, 3 * groups, groups)
    taps = jnp.pad(taps, ((0, 0), (0, 0), (0, groups), (0, 0)))
    weight = jnp.transpose(taps, (0, 3, 1, 2)).reshape(3 * groups, 12 * groups)
    return cost_mix(view_lists, warps, tiles, near, far, weight, groups)


def solution(mesh):
    return jax.shard_map(
        on_device,
        mesh=mesh,
        in_specs=(
            P("view", None, None),
            P("view", None),
            P(),
            P("view", None, None, "depth", None),
            P(),
        ),
        out_specs=P("view", None, "depth", None, None),
        check_vma=False,
    )
```

```python
import jax
import jax.numpy as jnp
from jax import lax
from jax.experimental import pallas as pl
from jax.experimental.pallas import tpu as pltpu
from jax.sharding import PartitionSpec as P

LOW = 256


def ask_kernel(requests_ref, tiles_ref, out_ref):
    here = lax.axis_index("view")
    count, slots, _, half = out_ref.shape
    start = pl.multiple_of((lax.axis_index("depth") % 2) * half, half)
    for u in range(count):
        for c in range(slots):
            out_ref[u, c] = tiles_ref[requests_ref[u, c, here], :, pl.ds(start, half)]


def asked_tiles(requests, tiles):
    askers, slots, _ = requests.shape
    _, channels, pixels = tiles.shape
    return pl.pallas_call(
        ask_kernel,
        in_specs=[pl.BlockSpec(memory_space=pltpu.SMEM), pl.BlockSpec(memory_space=pltpu.VMEM)],
        out_specs=pl.BlockSpec(memory_space=pltpu.VMEM),
        out_shape=jax.ShapeDtypeStruct((askers, slots, channels, pixels // 2), jnp.bfloat16),
        name="ask",
    )(requests, tiles)


def pack_kernel(warp_ref, *refs):
    *out_refs, rows_ref = refs
    views, sources, planes, _ = warp_ref.shape
    slabs = len(out_refs)
    slab = planes // slabs
    here = lax.axis_index("depth")
    for k, out_ref in enumerate(out_refs):
        t = (here + k) % slabs
        first = pl.multiple_of(t * slab, slab)
        before = jnp.maximum(first - 1, 0)
        after = jnp.minimum(first + slab, planes - 1)
        for v in range(views):
            for s in range(sources):
                r = s * (slab + 2)
                rows_ref[r + 1 : r + 1 + slab] = warp_ref[v, s, pl.ds(first, slab), :]
                rows_ref[r : r + 1] = jnp.where(t == 0, -1, warp_ref[v, s, pl.ds(before, 1), :])
                rows_ref[r + 1 + slab : r + 2 + slab] = jnp.where(
                    t == slabs - 1, -1, warp_ref[v, s, pl.ds(after, 1), :]
                )
            out_ref[v] = rows_ref[...].astype(jnp.int16)


def packed_warp(warp, slabs):
    views, sources, planes, columns = warp.shape
    rows = sources * (planes // slabs + 2)
    return pl.pallas_call(
        pack_kernel,
        in_specs=[pl.BlockSpec(memory_space=pltpu.VMEM)],
        out_specs=[pl.BlockSpec(memory_space=pltpu.VMEM)] * slabs,
        out_shape=[jax.ShapeDtypeStruct((views, rows, columns), jnp.int16)] * slabs,
        scratch_shapes=[pltpu.VMEM((rows, columns), jnp.int32)],
        cost_estimate=pl.CostEstimate(flops=warp.size, bytes_accessed=warp.size * 6, transcendentals=0),
        compiler_params=pltpu.CompilerParams(vmem_limit_bytes=8 << 20),
        name="pack",
    )(warp)


def cost_mix_kernel(slot_ref, *refs):
    warp_refs = refs[:-11]
    own_ref, near_ref, far_ref, weight_ref, out_ref = refs[-11:-6]
    low_ref, high_ref, scale_ref, sums_ref, taps_ref, rows_ref = refs[-6:]
    view = pl.program_id(0)
    rows = len(warp_refs)
    columns = warp_refs[0].shape[2]
    sources = slot_ref.shape[1]
    planes = warp_refs[0].shape[1] // sources
    channels = own_ref.shape[1]
    groups = out_ref.shape[1]
    size = channels // groups
    here = lax.axis_index("depth")
    flip = (here % 2) * 2

    for k in range(rows):
        i = (here + rows - k) % rows
        warp = warp_refs[k][0].astype(jnp.int32)
        outside = warp < 0
        low_ref[i] = jnp.where(outside, -1, warp & (LOW - 1)).astype(jnp.float32)
        high_ref[i] = (warp >> 8) ^ flip
        sums_ref[0 : sources * planes] = jnp.where(outside, 0.0, 1.0)
        live = sums_ref[0:planes]
        for s in range(1, sources):
            live = live + sums_ref[s * planes : (s + 1) * planes]
        scale_ref[i] = 0.5 / jnp.maximum(live, 1.0)

    tiles = LOW // 16
    pixel = lax.broadcasted_iota(jnp.int32, (tiles, 16, columns), 0) * 16 + lax.broadcasted_iota(
        jnp.int32, (tiles, 16, columns), 1
    )
    pixel = pixel.astype(jnp.float32).astype(jnp.bfloat16)
    one = jnp.ones((), jnp.bfloat16)
    zero = jnp.zeros((), jnp.bfloat16)
    lane = lax.broadcasted_iota(jnp.int32, (groups, columns), 1)
    blank = jnp.zeros((groups, columns), jnp.float32)

    for d in range(planes):
        totals = [jnp.zeros((channels, columns), jnp.float32) for _ in range(rows)]
        for s in range(sources):
            near = near_ref[slot_ref[view, s]]
            far = far_ref[slot_ref[view, s]]
            lhs = jnp.concatenate([near[:, :LOW], near[:, LOW:], far[:, :LOW], far[:, LOW:]], axis=0)
            hots = []
            for i in range(rows):
                row = jnp.broadcast_to(low_ref[i, pl.ds(s * planes + d, 1), :], (16, columns)).astype(jnp.bfloat16)
                hots.append(jnp.where(pixel == row[None], one, zero).reshape(LOW, columns))
            picked = jnp.dot(lhs, jnp.concatenate(hots, axis=1), preferred_element_type=jnp.float32)
            for i in range(rows):
                high = jnp.broadcast_to(high_ref[i, pl.ds(s * planes + d, 1), :], (channels, columns))
                odd = (high & 1) == 1
                upper = (high & 2) == 2
                part = picked[:, i * columns : (i + 1) * columns]
                q = [part[h * channels : (h + 1) * channels] for h in range(4)]
                totals[i] = totals[i] + jnp.where(upper, jnp.where(odd, q[3], q[2]), jnp.where(odd, q[1], q[0]))
        for i in range(rows):
            own = own_ref[0, :, i * columns : (i + 1) * columns].astype(jnp.float32)
            start = ((d % 2) * rows + i) * channels
            sums_ref[start : start + channels] = totals[i] * own
            corr = sums_ref[pl.ds(start, groups, stride=size), :]
            for n in range(1, size):
                corr = corr + sums_ref[pl.ds(start + n, groups, stride=size), :]
            cell = corr * jnp.broadcast_to(scale_ref[i, pl.ds(d, 1), :], (groups, columns))
            left = jnp.where(lane == 0, 0.0, pltpu.roll(cell, 1, 1))
            right = jnp.where(lane == columns - 1, 0.0, pltpu.roll(cell, columns - 1, 1))
            taps_ref[d, i] = jnp.concatenate([left, cell, right, blank], axis=0).astype(jnp.bfloat16)

    empty = jnp.zeros((4 * groups, columns), jnp.bfloat16)
    weight = weight_ref[...]
    terms = []
    for d in range(planes):
        taps = [taps_ref[d, i] for i in range(rows)]
        above = jnp.concatenate([empty] + taps[:-1], axis=1)
        below = jnp.concatenate(taps[1:] + [empty], axis=1)
        matrix = jnp.concatenate([above, jnp.concatenate(taps, axis=1), below], axis=0)
        terms.append(jnp.dot(weight, matrix, preferred_element_type=jnp.float32))
        if d >= 2:
            mixed = terms[d - 2][0:groups] + terms[d - 1][groups : 2 * groups] + terms[d][2 * groups : 3 * groups]
            for i in range(rows):
                rows_ref[pl.ds(i, groups, stride=rows), :] = mixed[:, i * columns : (i + 1) * columns]
            for h in range(groups):
                out_ref[0, h, d - 2] = rows_ref[h * rows : (h + 1) * rows, :].astype(jnp.bfloat16)


def cost_mix(slots, warps, tiles, near, far, weight, groups):
    rows = len(warps)
    views, sources = slots.shape
    columns = warps[0].shape[2]
    planes = warps[0].shape[1] // sources
    channels = tiles.shape[1]
    whole = {"pipeline_mode": pl.Buffered(1)}
    return pl.pallas_call(
        cost_mix_kernel,
        grid_spec=pltpu.PrefetchScalarGridSpec(
            num_scalar_prefetch=1,
            grid=(views,),
            in_specs=[pl.BlockSpec((1, sources * planes, columns), lambda v, s: (v, 0, 0))] * rows
            + [
                pl.BlockSpec((1, channels, tiles.shape[2]), lambda v, s: (v, 0, 0)),
                pl.BlockSpec(near.shape, lambda v, s: (0, 0, 0), **whole),
                pl.BlockSpec(far.shape, lambda v, s: (0, 0, 0), **whole),
                pl.BlockSpec(weight.shape, lambda v, s: (0, 0), **whole),
            ],
            out_specs=pl.BlockSpec((1, groups, planes - 2, rows, columns), lambda v, s: (v, 0, 0, 0, 0)),
            scratch_shapes=[
                pltpu.VMEM((rows, sources * planes, columns), jnp.float32),
                pltpu.VMEM((rows, sources * planes, columns), jnp.int32),
                pltpu.VMEM((rows, planes, columns), jnp.float32),
                pltpu.VMEM((2 * rows * channels, columns), jnp.float32),
                pltpu.VMEM((planes, rows, 4 * groups, columns), jnp.bfloat16),
                pltpu.VMEM((groups * rows, columns), jnp.float32),
            ],
        ),
        out_shape=jax.ShapeDtypeStruct((views, groups, planes - 2, rows, columns), jnp.bfloat16),
        compiler_params=pltpu.CompilerParams(vmem_limit_bytes=24 << 20),
        name="costmix",
    )(slots, *warps, tiles, near, far, weight)


def on_device(features, view_lists, requests, warp_idx, conv_weight):
    slabs = lax.axis_size("depth")
    groups = conv_weight.shape[1]
    tiles = jnp.transpose(features, (0, 2, 1))
    channels = tiles.shape[1]
    half = tiles.shape[2] // 2
    send = asked_tiles(jnp.transpose(requests, (0, 2, 1)), tiles)
    near = lax.all_to_all(send, "view", split_axis=0, concat_axis=0, tiled=True)
    near = near.reshape(-1, channels, half)
    warps = packed_warp(warp_idx.reshape(warp_idx.shape[:3] + warp_idx.shape[4:]), slabs)
    warps = [warps[0]] + [
        lax.ppermute(warps[k], "depth", [(i, (i + k) % slabs) for i in range(slabs)]) for k in range(1, slabs)
    ]
    near, *warps = lax.optimization_barrier((near, *warps))
    far = lax.ppermute(near, "depth", [(i, i ^ 1) for i in range(slabs)])
    taps = conv_weight.reshape(3, 3, 3 * groups, groups)
    taps = jnp.pad(taps, ((0, 0), (0, 0), (0, groups), (0, 0)))
    weight = jnp.transpose(taps, (0, 3, 1, 2)).reshape(3 * groups, 12 * groups)
    return cost_mix(view_lists, warps, tiles, near, far, weight, groups)


def solution(mesh):
    return jax.shard_map(
        on_device,
        mesh=mesh,
        in_specs=(
            P("view", None, None),
            P("view", None),
            P(),
            P("view", None, None, "depth", None),
            P(),
        ),
        out_specs=P("view", None, "depth", None, None),
        check_vma=False,
    )
```

```python
import jax
import jax.numpy as jnp
from jax import lax
from jax.experimental import pallas as pl
from jax.experimental.pallas import tpu as pltpu
from jax.sharding import PartitionSpec as P

LOW = 256


def ask_kernel(requests_ref, tiles_ref, out_ref):
    here = lax.axis_index("view")
    count, slots, _, half = out_ref.shape
    start = pl.multiple_of((lax.axis_index("depth") % 2) * half, half)
    for u in range(count):
        for c in range(slots):
            out_ref[u, c] = tiles_ref[requests_ref[u, c, here], :, pl.ds(start, half)]


def asked_tiles(requests, tiles):
    askers, slots, _ = requests.shape
    _, channels, pixels = tiles.shape
    return pl.pallas_call(
        ask_kernel,
        in_specs=[pl.BlockSpec(memory_space=pltpu.SMEM), pl.BlockSpec(memory_space=pltpu.VMEM)],
        out_specs=pl.BlockSpec(memory_space=pltpu.VMEM),
        out_shape=jax.ShapeDtypeStruct((askers, slots, channels, pixels // 2), jnp.bfloat16),
        name="ask",
    )(requests, tiles)


def pack_kernel(warp_ref, *refs):
    *out_refs, rows_ref = refs
    views, sources, planes, _ = warp_ref.shape
    slabs = len(out_refs)
    slab = planes // slabs
    here = lax.axis_index("depth")
    for k, out_ref in enumerate(out_refs):
        t = (here + k) % slabs
        first = pl.multiple_of(t * slab, slab)
        before = jnp.maximum(first - 1, 0)
        after = jnp.minimum(first + slab, planes - 1)
        for v in range(views):
            for s in range(sources):
                r = s * (slab + 2)
                rows_ref[r + 1 : r + 1 + slab] = warp_ref[v, s, pl.ds(first, slab), :]
                rows_ref[r : r + 1] = jnp.where(t == 0, -1, warp_ref[v, s, pl.ds(before, 1), :])
                rows_ref[r + 1 + slab : r + 2 + slab] = jnp.where(
                    t == slabs - 1, -1, warp_ref[v, s, pl.ds(after, 1), :]
                )
            out_ref[v] = rows_ref[...].astype(jnp.int16)


def packed_warp(warp, slabs):
    views, sources, planes, columns = warp.shape
    rows = sources * (planes // slabs + 2)
    return pl.pallas_call(
        pack_kernel,
        in_specs=[pl.BlockSpec(memory_space=pltpu.VMEM)],
        out_specs=[pl.BlockSpec(memory_space=pltpu.VMEM)] * slabs,
        out_shape=[jax.ShapeDtypeStruct((views, rows, columns), jnp.int16)] * slabs,
        scratch_shapes=[pltpu.VMEM((rows, columns), jnp.int32)],
        cost_estimate=pl.CostEstimate(flops=warp.size, bytes_accessed=warp.size * 6, transcendentals=0),
        compiler_params=pltpu.CompilerParams(vmem_limit_bytes=8 << 20),
        name="pack",
    )(warp)


def cost_mix_kernel(slot_ref, *refs):
    warp_refs = refs[:-11]
    own_ref, near_ref, far_ref, weight_ref, out_ref = refs[-11:-6]
    low_ref, high_ref, scale_ref, sums_ref, taps_ref, rows_ref = refs[-6:]
    view = pl.program_id(0)
    rows = len(warp_refs)
    columns = warp_refs[0].shape[2]
    sources = slot_ref.shape[1]
    planes = warp_refs[0].shape[1] // sources
    channels = own_ref.shape[1]
    groups = out_ref.shape[1]
    size = channels // groups
    here = lax.axis_index("depth")
    flip = (here % 2) * 2

    for k in range(rows):
        i = (here + rows - k) % rows
        warp = warp_refs[k][0].astype(jnp.int32)
        outside = warp < 0
        low_ref[i] = jnp.where(outside, -1, warp & (LOW - 1)).astype(jnp.float32)
        high_ref[i] = (warp >> 8) ^ flip
        sums_ref[0 : sources * planes] = jnp.where(outside, 0.0, 1.0)
        live = sums_ref[0:planes]
        for s in range(1, sources):
            live = live + sums_ref[s * planes : (s + 1) * planes]
        scale_ref[i] = 0.5 / jnp.maximum(live, 1.0)

    tiles = LOW // 16
    pixel = lax.broadcasted_iota(jnp.int32, (tiles, 16, columns), 0) * 16 + lax.broadcasted_iota(
        jnp.int32, (tiles, 16, columns), 1
    )
    pixel = pixel.astype(jnp.float32).astype(jnp.bfloat16)
    one = jnp.ones((), jnp.bfloat16)
    zero = jnp.zeros((), jnp.bfloat16)
    lane = lax.broadcasted_iota(jnp.int32, (groups, columns), 1)
    blank = jnp.zeros((groups, columns), jnp.float32)

    for d in range(planes):
        totals = [jnp.zeros((channels, columns), jnp.float32) for _ in range(rows)]
        for s in range(sources):
            near = near_ref[slot_ref[view, s]]
            far = far_ref[slot_ref[view, s]]
            lhs = jnp.concatenate([near[:, :LOW], near[:, LOW:], far[:, :LOW], far[:, LOW:]], axis=0)
            hots = []
            for i in range(rows):
                row = jnp.broadcast_to(low_ref[i, pl.ds(s * planes + d, 1), :], (16, columns)).astype(jnp.bfloat16)
                hots.append(jnp.where(pixel == row[None], one, zero).reshape(LOW, columns))
            picked = jnp.dot(lhs, jnp.concatenate(hots, axis=1), preferred_element_type=jnp.float32)
            for i in range(rows):
                high = jnp.broadcast_to(high_ref[i, pl.ds(s * planes + d, 1), :], (channels, columns))
                odd = (high & 1) == 1
                upper = (high & 2) == 2
                part = picked[:, i * columns : (i + 1) * columns]
                q = [part[h * channels : (h + 1) * channels] for h in range(4)]
                totals[i] = totals[i] + jnp.where(upper, jnp.where(odd, q[3], q[2]), jnp.where(odd, q[1], q[0]))
        for i in range(rows):
            own = own_ref[0, :, i * columns : (i + 1) * columns].astype(jnp.float32)
            start = ((d % 2) * rows + i) * channels
            sums_ref[start : start + channels] = totals[i] * own
            corr = sums_ref[pl.ds(start, groups, stride=size), :]
            for n in range(1, size):
                corr = corr + sums_ref[pl.ds(start + n, groups, stride=size), :]
            cell = corr * jnp.broadcast_to(scale_ref[i, pl.ds(d, 1), :], (groups, columns))
            left = jnp.where(lane == 0, 0.0, pltpu.roll(cell, 1, 1))
            right = jnp.where(lane == columns - 1, 0.0, pltpu.roll(cell, columns - 1, 1))
            taps_ref[d, i] = jnp.concatenate([left, cell, right, blank], axis=0).astype(jnp.bfloat16)

    empty = jnp.zeros((4 * groups, columns), jnp.bfloat16)
    weight = weight_ref[...]
    terms = []
    for d in range(planes):
        taps = [taps_ref[d, i] for i in range(rows)]
        above = jnp.concatenate([empty] + taps[:-1], axis=1)
        below = jnp.concatenate(taps[1:] + [empty], axis=1)
        matrix = jnp.concatenate([above, jnp.concatenate(taps, axis=1), below], axis=0)
        terms.append(jnp.dot(weight, matrix, preferred_element_type=jnp.float32))
        if d >= 2:
            mixed = terms[d - 2][0:groups] + terms[d - 1][groups : 2 * groups] + terms[d][2 * groups : 3 * groups]
            for i in range(rows):
                rows_ref[pl.ds(i, groups, stride=rows), :] = mixed[:, i * columns : (i + 1) * columns]
            for h in range(groups):
                out_ref[0, h, d - 2] = rows_ref[h * rows : (h + 1) * rows, :].astype(jnp.bfloat16)


def cost_mix(slots, warps, tiles, near, far, weight, groups):
    rows = len(warps)
    views, sources = slots.shape
    columns = warps[0].shape[2]
    planes = warps[0].shape[1] // sources
    channels = tiles.shape[1]
    whole = {"pipeline_mode": pl.Buffered(1)}
    near, far = (pltpu.with_memory_space_constraint(part, pltpu.VMEM) for part in (near, far))
    return pl.pallas_call(
        cost_mix_kernel,
        grid_spec=pltpu.PrefetchScalarGridSpec(
            num_scalar_prefetch=1,
            grid=(views,),
            in_specs=[pl.BlockSpec((1, sources * planes, columns), lambda v, s: (v, 0, 0))] * rows
            + [
                pl.BlockSpec((1, channels, tiles.shape[2]), lambda v, s: (v, 0, 0)),
                pl.BlockSpec(memory_space=pltpu.VMEM),
                pl.BlockSpec(memory_space=pltpu.VMEM),
                pl.BlockSpec(weight.shape, lambda v, s: (0, 0), **whole),
            ],
            out_specs=pl.BlockSpec((1, groups, planes - 2, rows, columns), lambda v, s: (v, 0, 0, 0, 0)),
            scratch_shapes=[
                pltpu.VMEM((rows, sources * planes, columns), jnp.float32),
                pltpu.VMEM((rows, sources * planes, columns), jnp.int32),
                pltpu.VMEM((rows, planes, columns), jnp.float32),
                pltpu.VMEM((2 * rows * channels, columns), jnp.float32),
                pltpu.VMEM((planes, rows, 4 * groups, columns), jnp.bfloat16),
                pltpu.VMEM((groups * rows, columns), jnp.float32),
            ],
        ),
        out_shape=jax.ShapeDtypeStruct((views, groups, planes - 2, rows, columns), jnp.bfloat16),
        compiler_params=pltpu.CompilerParams(
            vmem_limit_bytes=24 << 20,
        ),
        name="costmix",
    )(slots, *warps, tiles, near, far, weight)


def on_device(features, view_lists, requests, warp_idx, conv_weight):
    slabs = lax.axis_size("depth")
    groups = conv_weight.shape[1]
    tiles = jnp.transpose(features, (0, 2, 1))
    channels = tiles.shape[1]
    half = tiles.shape[2] // 2
    send = asked_tiles(jnp.transpose(requests, (0, 2, 1)), tiles)
    near = lax.all_to_all(send, "view", split_axis=0, concat_axis=0, tiled=True)
    near = near.reshape(-1, channels, half)
    warps = packed_warp(warp_idx.reshape(warp_idx.shape[:3] + warp_idx.shape[4:]), slabs)
    warps = [warps[0]] + [
        lax.ppermute(warps[k], "depth", [(i, (i + k) % slabs) for i in range(slabs)]) for k in range(1, slabs)
    ]
    near, *warps = lax.optimization_barrier((near, *warps))
    far = lax.ppermute(near, "depth", [(i, i ^ 1) for i in range(slabs)])
    taps = conv_weight.reshape(3, 3, 3 * groups, groups)
    taps = jnp.pad(taps, ((0, 0), (0, 0), (0, groups), (0, 0)))
    weight = jnp.transpose(taps, (0, 3, 1, 2)).reshape(3 * groups, 12 * groups)
    return cost_mix(view_lists, warps, tiles, near, far, weight, groups)


def solution(mesh):
    return jax.shard_map(
        on_device,
        mesh=mesh,
        in_specs=(
            P("view", None, None),
            P("view", None),
            P(),
            P("view", None, None, "depth", None),
            P(),
        ),
        out_specs=P("view", None, "depth", None, None),
        check_vma=False,
    )
```
